32 devices in a mesh: cand: 2 (over x), row: 16 (over z, y, core).
Axes of the slice: x: 2, y: 2, z: 4, core: 2. Of those that a mesh axis runs over, the one named last changes fastest.
Arguments:
- coeffs: int32 [64], P('cand'), parts along dimension 0, may hold values from -1536 to 1536
- hidden_in: bfloat16 [512, 8192], P(None, 'row'), may hold values from -6 to 6
- gate_w: bfloat16 [8192, 14336], P(None, 'row'), may hold values from -0.0625 to 0.0625
- up_w: bfloat16 [8192, 14336], P(None, 'row'), may hold values from -0.0625 to 0.0625
- down_w: bfloat16 [14336, 8192], P('row'), may hold values from -0.046875 to 0.046875
- gate_a: bfloat16 [8192, 512], P('row'), may hold values from -6 to 6
- gate_b: bfloat16 [512, 14336], P(None, 'row'), may hold values from -0.0012207031 to 0.0012207031
- up_a: bfloat16 [8192, 512], P('row'), may hold values from -6 to 6
- up_b: bfloat16 [512, 14336], P(None, 'row'), may hold values from -0.0012207031 to 0.0012207031
- down_a: bfloat16 [14336, 512], P('row'), may hold values from -6 to 6
- down_bt: bfloat16 [8192, 512], P('row'), may hold values from -0.0009765625 to 0.0009765625
Outputs:
- layer_out: bfloat16 [1024, 8192], P('cand', 'row'), parts along dimension 0
The draws below stay inside these ranges and needn't reach their ends.
There are 2 independent parts, one for each index of `cand`. The reference program is written for one: setup_inputs(seed, part) draws one part's arguments, and reference() takes and returns one part's arrays. A program takes and returns all parts, laid end to end along the dimension named above; an argument that names none is the same for every part. Nothing has to cross between parts.
All inputs are finite; a program needn't handle non-finite values.
Results may differ from the reference program's by a relative error of at most 0.0055.
Values may be sent and summed in bfloat16 or wider, within the bound.
No kernel may reach another device: no remote copies, remote signals or barrier semaphores. Data moves between devices by JAX's collectives and lax.ppermute only.
A program may use at most 128 MiB of HBM per device.

```python
import jax
import jax.numpy as jnp
from jax import lax

D = 8192
FF = 14336
MODULES = 32
RANK = 16
TOK = 512
R = 512


def touch_ends(result, own_key, smallest, largest):
    spot = [jax.random.randint(jax.random.fold_in(own_key, axis), (), 0, length) for axis, length in enumerate(result.shape)]
    longest = result.shape.index(max(result.shape))
    next_to = spot[:longest] + [(spot[longest] + 1) % result.shape[longest]] + spot[longest + 1:]
    return result.at[tuple(spot)].set(smallest).at[tuple(next_to)].set(largest)


def shard_levels(stream_key, extent, shards, least, top_value):
    gain = 1.0
    for axis_at, shards_of in shards:
        steps = jax.random.uniform(jax.random.fold_in(jax.random.fold_in(stream_key, 6), axis_at), (shards_of,), jnp.float32, least / len(shards), top_value / len(shards))
        gain = gain * jnp.repeat(jnp.exp(steps), extent[axis_at] // shards_of).reshape((-1,) + (1,) * (len(extent) - 1 - axis_at))
    return gain


def noise(key, dims, deviation, most, pieces=(), dtype=jnp.bfloat16):
    factor_of = shard_levels(key, dims, pieces, -0.22, 0.18) if pieces else 1.0
    array = jax.random.normal(key, dims, jnp.float32) * deviation * factor_of
    return jnp.minimum(jnp.maximum(array, -most), most).astype(dtype)


def setup_inputs(seed: int = 0, part: int = 0) -> dict:
    splits = jax.random.split(jax.random.key(seed), 12)
    part_keys = jax.random.split(jax.random.fold_in(splits[11], part), 12)
    return {
        "coeffs": touch_ends(jax.random.randint(part_keys[0], (MODULES,), -1536, 1537), jax.random.fold_in(part_keys[0], 1), -1536, 1536).astype(jnp.int32),
        "hidden_in": noise(splits[1], (TOK, D), 1.0, 6.0, ((1, 16),)),
        "gate_w": noise(splits[2], (D, FF), D ** -0.5, 0.0625, ((1, 16),)),
        "up_w": noise(splits[3], (D, FF), D ** -0.5, 0.0625, ((1, 16),)),
        "down_w": noise(splits[4], (FF, D), FF ** -0.5, 0.046875, ((0, 16),)),
        "gate_a": noise(splits[5], (D, R), 1.0, 6.0, ((0, 16),)),
        "gate_b": noise(splits[6], (R, FF), (6 * R * D) ** -0.5, 0.0012207031, ((1, 16),)),
        "up_a": noise(splits[7], (D, R), 1.0, 6.0, ((0, 16),)),
        "up_b": noise(splits[8], (R, FF), (6 * R * D) ** -0.5, 0.0012207031, ((1, 16),)),
        "down_a": noise(splits[9], (FF, R), 1.0, 6.0, ((0, 16),)),
        "down_bt": noise(splits[10], (D, R), (6 * R * FF) ** -0.5, 0.0009765625, ((0, 16),)),
    }


def reference(coeffs, hidden_in, gate_w, up_w, down_w, gate_a, gate_b, up_a, up_b, down_a, down_bt):
    weights_r = jnp.repeat(coeffs.astype(jnp.float32) / 1024.0, RANK)
    scaled_gate = (gate_b.astype(jnp.float32) * weights_r[:, None]).astype(jnp.bfloat16)
    scaled_up = (up_b.astype(jnp.float32) * weights_r[:, None]).astype(jnp.bfloat16)
    scaled_down = (down_a.astype(jnp.float32) * weights_r[None, :]).astype(jnp.bfloat16)
    highest = lax.Precision.HIGHEST
    low_gate = jnp.dot(hidden_in, gate_a, preferred_element_type=jnp.float32)
    low_up = jnp.dot(hidden_in, up_a, preferred_element_type=jnp.float32)
    gate_act = jnp.dot(hidden_in, gate_w, preferred_element_type=jnp.float32) + jnp.dot(low_gate, scaled_gate.astype(jnp.float32), precision=highest)
    up_act = jnp.dot(hidden_in, up_w, preferred_element_type=jnp.float32) + jnp.dot(low_up, scaled_up.astype(jnp.float32), precision=highest)
    hidden = (jax.nn.silu(gate_act) * up_act).astype(jnp.bfloat16)
    low_down = jnp.dot(hidden, scaled_down, preferred_element_type=jnp.float32)
    extra = lax.dot_general(low_down, down_bt.astype(jnp.float32), (((1,), (1,)), ((), ())), precision=highest)
    base = jnp.dot(hidden, down_w, preferred_element_type=jnp.float32)
    return (base + extra).astype(jnp.bfloat16)
```

```python
import jax
import jax.numpy as jnp
from jax import lax
from jax.experimental import pallas as pl
from jax.experimental.pallas import tpu as pltpu
from jax.sharding import PartitionSpec as P


F32 = jnp.float32
BF16 = jnp.bfloat16
CORES = 2


def ring_order(mesh):
    devices = mesh.devices[0]
    chips = len(devices) // CORES
    coords = [getattr(devices[i * CORES], "coords", None) for i in range(chips)]
    if any(c is None for c in coords):
        return list(range(chips))
    coords = [tuple(c) for c in coords]
    moving = [a for a in range(len(coords[0])) if len({c[a] for c in coords}) > 1]
    narrow = [a for a in moving if len({c[a] for c in coords}) == 2]
    if len(moving) != 2 or not narrow:
        return list(range(chips))
    short = narrow[-1]
    long = [a for a in moving if a != short][0]
    low = min(c[short] for c in coords)
    near = sorted((c[long], i) for i, c in enumerate(coords) if c[short] == low)
    far = sorted((c[long], i) for i, c in enumerate(coords) if c[short] != low)
    return [i for _, i in near] + [i for _, i in reversed(far)]


def gate_up(acc, blocks, chips, gate_w, up_w):
    count = len(blocks)
    rows, width = blocks[0].shape
    ff = gate_w.shape[1]
    per = 2
    deep = width // per

    def kernel(chips_ref, *refs):
        xs, weights, rest = refs[:count], refs[count : count + 2], refs[count + 2 :]
        starts, outs = (rest[:2], rest[2:]) if acc else (None, rest)
        for at in range(count * per):

            @pl.when(pl.program_id(0) == at)
            def _():
                x = xs[at // per][:, at % per * deep : (at % per + 1) * deep]
                for i, (w, o) in enumerate(zip(weights, outs)):
                    y = jnp.dot(x, w[...], preferred_element_type=F32)
                    if at:
                        o[...] += y
                    else:
                        o[...] = starts[i][...] + y if acc else y

    whole = pl.BlockSpec((rows, ff), lambda i, chips: (0, 0))
    weight = pl.BlockSpec((deep, ff), lambda i, chips: (chips[i // per] * per + i % per, 0))
    shape = jax.ShapeDtypeStruct((rows, ff), F32)
    return pl.pallas_call(
        kernel,
        grid_spec=pltpu.PrefetchScalarGridSpec(
            num_scalar_prefetch=1,
            grid=(count * per,),
            in_specs=[pl.BlockSpec((rows, width), lambda i, chips: (0, 0))] * count
            + [weight] * 2
            + ([whole] * 2 if acc else []),
            out_specs=[whole] * 2,
        ),
        out_shape=[shape] * 2,
        compiler_params=pltpu.CompilerParams(dimension_semantics=("arbitrary",)),
        cost_estimate=pl.CostEstimate(
            flops=4 * count * rows * width * ff,
            bytes_accessed=4 * count * width * ff + 16 * rows * ff,
            transcendentals=0,
        ),
        name="gate_up",
    )(chips, *blocks, gate_w, up_w, *(acc or ()))


def build(mesh):
    order = ring_order(mesh)
    n = len(order)
    place = {chip: at for at, chip in enumerate(order)}
    half = n // 2
    planes = mesh.shape["cand"]

    def chip_at(chip, k):
        return order[(place[chip] + k) % n]

    forth = [(i * CORES + c, chip_at(i, 1 - 2 * c) * CORES + c) for i in range(n) for c in range(CORES)]
    pair = [(i, i ^ 1) for i in range(n * CORES)]
    table = [[chip_at(i, (1 - 2 * c) * k) for k in range(n)] for i in range(n) for c in range(CORES)]

    def send(v, perm):
        return lax.ppermute(v, "row", perm)

    def by_core(core, mine, other, axis):
        return jnp.where(
            core == 0, jnp.concatenate([mine, other], axis), jnp.concatenate([other, mine], axis)
        )

    def half_of(v, at, axis):
        size = v.shape[axis] // 2
        return lax.dynamic_slice_in_dim(v, at * size, size, axis)

    def chip_pair(bit):
        return [(i * CORES + c, (i ^ bit) * CORES + c) for i in range(n) for c in range(CORES)]

    def row_sum(v, row):
        core, chip = row % CORES, row // CORES
        given = half_of(v, 1 - core, 0).astype(BF16)
        v = half_of(v, core, 0) + send(given, pair).astype(F32)
        bits = [1 << b for b in range(n.bit_length() - 1)]
        for bit in bits:
            at = (chip // bit) % 2
            given = half_of(v, 1 - at, 0).astype(BF16)
            kept = half_of(v, at, 0)
            given, kept = yield given, kept
            v = kept + send(given, chip_pair(bit)).astype(F32)
        v = v.astype(BF16)
        for bit in reversed(bits):
            (v,) = yield (v,)
            v = by_core((chip // bit) % 2, v, send(v, chip_pair(bit)), 0)
        yield by_core(core, v, send(v, pair), 0)

    def after(*groups):
        leaves, tree = jax.tree.flatten(groups)
        return jax.tree.unflatten(tree, lax.optimization_barrier(leaves))

    class Side:
        def __init__(self, v, row):
            self.steps = row_sum(v, row)
            self.state = next(self.steps)
            self.left = 2 * (n.bit_length() - 1)

        def go(self, count):
            for _ in range(min(count, self.left)):
                self.state = self.steps.send(self.state)
                self.left -= 1

        def result(self):
            self.go(self.left)
            return self.state

    def shards(coeffs, hidden_in, gate_w, up_w, down_w, gate_a, gate_b, up_a, up_b, down_a, down_bt):
        modules, ranks = coeffs.shape[0], gate_b.shape[0]
        cand = lax.axis_index("cand")
        row = lax.axis_index("row")
        core = row % CORES
        ahead = jnp.asarray(table, jnp.int32)[row]
        tokens = hidden_in.shape[0] // planes
        width = hidden_in.shape[1] * CORES
        ff = gate_w.shape[1]
        steps = 2 * (n.bit_length() - 1)

        def product(acc, blocks, chips):
            return gate_up(acc, blocks, jnp.stack(chips), gate_w, up_w)

        hid = lax.dynamic_slice_in_dim(hidden_in, cand * tokens, tokens, 0)
        block = by_core(core, hid, send(hid, pair), 1)
        side = Side(
            jnp.concatenate(
                [
                    jnp.dot(hid, gate_a, preferred_element_type=F32),
                    jnp.dot(hid, up_a, preferred_element_type=F32),
                ],
                1,
            ),
            row,
        )

        scaled = []
        where_r = lambda axis: lax.broadcasted_iota(jnp.int32, (ranks, modules), axis)
        member = where_r(0) // (ranks // modules) == where_r(1)
        for j in range(1, planes + 1):
            mine = coeffs
            if j < planes:
                mine = lax.ppermute(coeffs, "cand", [((i + j) % planes, i) for i in range(planes)])
            spread = jnp.where(member, mine.astype(F32)[None, :] / 1024.0, 0.0)
            weights = jnp.sum(spread, 1)
            scaled.append(
                (
                    (gate_b.astype(F32) * weights[:, None]).astype(BF16),
                    (up_b.astype(F32) * weights[:, None]).astype(BF16),
                    (down_a.astype(F32) * weights[None, :]).astype(BF16),
                )
            )

        acc = None
        own = (block,), (ahead[0],)
        for k in range(1, half + 1):
            got = send(half_of(block, core, 0) if k == half else block, forth)
            if k == 1:
                acc = product(acc, *own)
            else:
                acc = product(acc, (block, send(block, pair)), (ahead[n - k + 1], ahead[k - 1]))
            side.go(steps * k // half - steps * (k - 1) // half)
            got, acc, side.state, scaled = after(got, acc, side.state, scaled)
            block = got
        last = by_core(core, block, send(block, pair), 0)
        low = side.result()
        low_gate, low_up = low[:, :ranks], low[:, ranks:]
        gate, up = product(acc, (last,), (ahead[half],))

        hidden = []
        low_down = []
        for s_gate, s_up, s_down in scaled:
            gate_act = gate + jnp.dot(low_gate, s_gate, preferred_element_type=F32)
            up_act = up + jnp.dot(low_up, s_up, preferred_element_type=F32)
            h = (jax.nn.silu(gate_act) * up_act).astype(BF16)
            hidden.append(h)
            low_down.append(jnp.dot(h, s_down, preferred_element_type=F32))
        hidden = jnp.concatenate(hidden, 0)
        side = Side(jnp.concatenate(low_down, 0), row)

        rows = hidden.shape[0]
        groups = 2
        size = rows // groups
        parts = [hidden[i * size : (i + 1) * size] for i in range(groups)]

        def down(h, chip):
            w = lax.dynamic_slice_in_dim(down_w, chip * width, width, 1)
            return jnp.dot(h, w, preferred_element_type=F32)

        def chip_sum(h, k):
            other = send(down(h, ahead[n - k]).astype(BF16), pair)
            return down(h, ahead[k]) + other.astype(F32)

        full = down(hidden, ahead[half])
        mine = jnp.concatenate([half_of(full[i * size : (i + 1) * size], core, 0) for i in range(groups)], 0)
        given = jnp.concatenate([half_of(full[i * size : (i + 1) * size], 1 - core, 0) for i in range(groups)], 0)
        far = (mine + send(given.astype(BF16), pair).astype(F32)).astype(BF16)
        far = send(far, forth)
        sums = [chip_sum(h, half - 1) for h in parts]
        side.go(1)
        far, sums, side.state = after(far, sums, side.state)
        held = []
        for i in range(groups):
            got = far[i * size // 2 : (i + 1) * size // 2].astype(F32)
            held.append((by_core(core, got, jnp.zeros_like(got), 0) + sums[i]).astype(BF16))
        flying = [send(m, forth) for m in held]
        done = [None] * groups
        for k in range(half - 2, -1, -1):
            for i, h in enumerate(parts):
                ready = chip_sum(h, k) if k else down(h, ahead[0])
                side.go(1)
                got, ready, side.state = after(flying[i], ready, side.state)
                got = got.astype(F32) + ready
                if k:
                    flying[i] = send(got.astype(BF16), forth)
                else:
                    done[i] = half_of(got, core, 1) + send(half_of(got, 1 - core, 1), pair)
        extra = lax.dot_general(
            side.result(), down_bt, (((1,), (1,)), ((), ())), preferred_element_type=F32
        )
        out = jnp.zeros((planes * tokens, down_bt.shape[0]), BF16)
        done = [(done[i] + extra[i * size : (i + 1) * size]).astype(BF16) for i in range(groups)]
        for j in range(1, planes + 1):
            at = (j - 1) * tokens
            piece = done[at // size][at % size : at % size + tokens] if tokens <= size else jnp.concatenate(done, 0)
            if j < planes:
                piece = lax.ppermute(piece, "cand", [(i, (i + j) % planes) for i in range(planes)])
            out = lax.dynamic_update_slice_in_dim(out, piece, (cand - j) % planes * tokens, 0)
        return out

    return shards


def solution(mesh):
    in_specs = (
        P("cand"),
        P(None, "row"),
        P(None, "row"),
        P(None, "row"),
        P("row", None),
        P("row", None),
        P(None, "row"),
        P("row", None),
        P(None, "row"),
        P("row", None),
        P("row", None),
    )
    out_specs = P("cand", "row")
    return jax.shard_map(build(mesh), mesh=mesh, in_specs=in_specs, out_specs=out_specs, check_vma=False)
```
